256 devices in a mesh: ctx: 16 (over y, x), grp: 8 (over z), side: 2 (over core).
Axes of the slice: x: 4, y: 4, z: 8, core: 2. Of those that a mesh axis runs over, the one named last changes fastest.
Arguments:
- tokens: bfloat16 [4096, 2048], P(('ctx', 'grp', 'side')), may hold values from -6 to 6
- norm_gain: float32 [2048], replicated, may hold values from 0.25 to 1.75
- combine: float32 [4096, 8], P(('ctx', 'grp', 'side')), may hold values from 0.05 to 0.6
- expert_ids: int32 [4096, 8], P(('ctx', 'grp', 'side')), may hold values from 0 to 127, all different within a row; in each aligned block of 16 rows (0 to 15, 16 to 31, ...) at most 2 rows name the same one
- w_gate: bfloat16 [128, 2048, 768], P(('ctx', 'grp'), None, 'side'), may hold values from -0.125 to 0.125
- w_up: bfloat16 [128, 2048, 768], P(('ctx', 'grp'), None, 'side'), may hold values from -0.125 to 0.125
- w_down: bfloat16 [128, 768, 2048], P(('ctx', 'grp'), 'side'), may hold values from -0.21875 to 0.21875
- d_out: bfloat16 [4096, 2048], P(('ctx', 'grp', 'side')), may hold values from -6 to 6
Outputs:
- mixed: bfloat16 [4096, 2048], P(('ctx', 'grp', 'side'))
- d_tokens: bfloat16 [4096, 2048], P(('ctx', 'grp', 'side'))
- d_gain: float32 [2048], replicated
- d_combine: float32 [4096, 8], P(('ctx', 'grp', 'side'))
- d_w_gate: bfloat16 [128, 2048, 768], P(('ctx', 'grp'), None, 'side')
- d_w_up: bfloat16 [128, 2048, 768], P(('ctx', 'grp'), None, 'side')
- d_w_down: bfloat16 [128, 768, 2048], P(('ctx', 'grp'), 'side')
The draws below stay inside these ranges and needn't reach their ends.
Inputs may be any that keep to these rules, and one draw needn't show every extreme that they name: `expert_ids`: each row names 8 different experts; among the 16 rows of one device no expert is named more than 2 times, and that bound is reached.
All inputs are finite; a program needn't handle non-finite values.
Results may differ from the reference program's by a relative error of at most 0.0072.
Values may be sent and summed in bfloat16 or wider, within the bound.
No kernel may reach another device: no remote copies, remote signals or barrier semaphores. Data moves between devices by JAX's collectives and lax.ppermute only.
A program may use at most 128 MiB of HBM per device.

```python
import math
import jax
import jax.numpy as jnp
import numpy as np
from jax import lax

D = 2048
FF = 768
TOP = 8
TOK_DEV = 16
EXPERTS = 128
TOKENS = 4096
SLOTS = 2


def steps_of(stream_key, dims, cuts, low, top_value):
    def one(axis_at, parts):
        steps = jax.random.uniform(jax.random.fold_in(jax.random.fold_in(stream_key, 6), axis_at), (parts,), jnp.float32, low / len(cuts), top_value / len(cuts))
        return jnp.repeat(jnp.exp(steps), dims[axis_at] // parts).reshape((-1,) + (1,) * (len(dims) - axis_at - 1))

    factor_of = one(*cuts[0])
    for cut in cuts[1:]:
        factor_of = factor_of * one(*cut)
    return factor_of


def assign_block(key, own, number, rows, number_of, top, bound, skew):
    order = jax.random.permutation(key, number_of)
    heavy_load, ordinary = load_shares(number_of, rows * top, bound, skew, True), load_shares(number_of, rows * top, bound, skew, False)
    places = jnp.arange(number_of)

    def named(sizes, rotation):
        used = int((sizes > 0).sum())
        fixed = max(1, used // 4)
        shifted = fixed + (places - fixed + rotation * (used - fixed)) % max(1, number_of - fixed)
        return jnp.zeros((number_of,), jnp.int32).at[order[jnp.where(places < fixed, places, shifted)]].set(jnp.asarray(sizes, jnp.int32))

    sizes = jnp.where(number % 4 == 0, named(heavy_load, number // 4), named(ordinary, number - number // 4 - 1))
    mixed = jax.random.permutation(jax.random.fold_in(own, 3), number_of)
    giver, sink = mixed[0:number_of // 2 * 2:2], mixed[1:number_of // 2 * 2:2]
    room = jnp.minimum(sizes[giver] - 1, bound - sizes[sink]) // 2
    room = jnp.where((giver == order[0]) | (sink == order[0]) | (sizes[sink] == 0), 0, jnp.maximum(room, 0))
    shifted = jax.random.randint(jax.random.fold_in(own, 4), (number_of // 2,), 0, 1 << 20) % (room + 1)
    sizes = sizes.at[giver].add(-shifted).at[sink].add(shifted)
    members = jnp.searchsorted(jnp.cumsum(sizes), jnp.arange(rows * top), side="right").astype(jnp.int32)
    table = members.reshape(top, rows).T
    table = table[jax.random.permutation(jax.random.fold_in(own, 1), rows)]
    rotation = jax.random.randint(jax.random.fold_in(own, 2), (rows, 1), 0, top)
    return jnp.take_along_axis(table, (jnp.arange(top)[None, :] + rotation) % top, axis=1)


def load_shares(amount, total, limit, lean, full):
    loads = [(1 << 20) // math.isqrt(rank ** lean) + 1 for rank in range(1, amount + 1)]
    largest = limit if full else min(limit, max(-(-total // amount), total * loads[0] // sum(loads)))
    least = 1 if total - largest >= amount - 1 else 0
    counts, spare = [largest] + [least] * (amount - 1), total - largest - least * (amount - 1)
    while spare > 0:
        movable = [i for i in range(1, amount) if counts[i] < largest] or [i for i in range(1, amount) if counts[i] < limit]
        mass, left = sum([loads[i] for i in movable]), spare
        for i in movable:
            extra = min(limit - counts[i], max(1, left * loads[i] // mass), spare)
            counts[i] = counts[i] + extra
            spare = spare - extra
    return np.array(counts)


def gaussian(own_key, shape, spread, reach, split=(), kind=jnp.bfloat16):
    result = spread * jax.random.normal(own_key, shape, jnp.float32)
    if split:
        result = result * steps_of(own_key, shape, split, -0.22, 0.18)
    return jnp.clip(result, -reach, reach).astype(kind)


def setup_inputs(seed: int = 0) -> dict:
    key_list = jax.random.split(jax.random.key(seed), 9)
    tokens = gaussian(key_list[0], (TOKENS, D), 1.0, 6.0, ((0, 256),))
    norm_gain = jnp.clip(1.0 + 0.15 * jax.random.normal(key_list[1], (D,), jnp.float32), 0.25, 1.75)
    combine = jnp.clip(jnp.exp(math.log(0.6) - 2.4849067 * jax.random.uniform(key_list[2], (TOKENS, TOP), jnp.float32) ** steps_of(key_list[2], (TOKENS, TOP), ((0, 256),), -0.2, 0.2)), 0.05, 0.6)
    expert_ids_keys = jax.random.split(jax.random.fold_in(key_list[3], 1), TOKENS // TOK_DEV)
    expert_ids_turns = jax.random.permutation(jax.random.fold_in(key_list[3], 3), TOKENS // TOK_DEV)
    expert_ids = jax.vmap(lambda own, number: assign_block(jax.random.fold_in(key_list[3], 2), own, number, TOK_DEV, EXPERTS, TOP, SLOTS, 2))(expert_ids_keys, expert_ids_turns).reshape((TOKENS, TOP))
    w_gate = gaussian(key_list[4], (EXPERTS, D, FF), D ** -0.5, 0.125, ((0, 128), (2, 2)))
    w_up = gaussian(key_list[5], (EXPERTS, D, FF), D ** -0.5, 0.125, ((0, 128), (2, 2)))
    w_down = gaussian(key_list[6], (EXPERTS, FF, D), FF ** -0.5, 0.21875, ((0, 128), (1, 2)))
    d_out = gaussian(key_list[7], (TOKENS, D), 1.0, 6.0, ((0, 256),))
    return dict(tokens=tokens, norm_gain=norm_gain, combine=combine, expert_ids=expert_ids, w_gate=w_gate, w_up=w_up, w_down=w_down, d_out=d_out)


EPS = 1e-06

def expert_pass(rows, grads, gate_w, up_w, down_w):
    a_gate = jnp.dot(rows, gate_w, preferred_element_type=jnp.float32)
    a_up = jnp.dot(rows, up_w, preferred_element_type=jnp.float32)
    sigmoid_gate = jax.nn.sigmoid(a_gate)
    silu_gate = a_gate * sigmoid_gate
    hidden = (silu_gate * a_up).astype(jnp.bfloat16)
    output = jnp.dot(hidden, down_w, preferred_element_type=jnp.float32)
    d_hidden = lax.dot_general(grads, down_w, (((1,), (1,)), ((), ())), preferred_element_type=jnp.float32)
    d_up = (d_hidden * silu_gate).astype(jnp.bfloat16)
    d_gate = (d_hidden * a_up * sigmoid_gate * (1.0 + a_gate * (1.0 - sigmoid_gate))).astype(jnp.bfloat16)
    d_rows = lax.dot_general(d_gate, gate_w, (((1,), (1,)), ((), ())), preferred_element_type=jnp.float32)
    d_rows = d_rows + lax.dot_general(d_up, up_w, (((1,), (1,)), ((), ())), preferred_element_type=jnp.float32)
    g_gate = lax.dot_general(rows, d_gate, (((0,), (0,)), ((), ())), preferred_element_type=jnp.float32)
    g_up = lax.dot_general(rows, d_up, (((0,), (0,)), ((), ())), preferred_element_type=jnp.float32)
    g_down = lax.dot_general(hidden, grads, (((0,), (0,)), ((), ())), preferred_element_type=jnp.float32)
    return (output, d_rows, g_gate, g_up, g_down)

def row_table(expert_ids):
    blocks = TOKENS // TOK_DEV
    flat_ids = expert_ids.reshape(blocks, TOK_DEV * TOP).astype(jnp.int32)
    onehot = (flat_ids[:, :, None] == jnp.arange(EXPERTS, dtype=jnp.int32)[None, None, :]).astype(jnp.int32)
    before = jnp.cumsum(onehot, axis=1) - onehot
    slot = lax.optimization_barrier(jnp.sum(before * onehot, axis=2)).astype(jnp.int32)
    block_ids = jnp.arange(blocks, dtype=jnp.int32)[:, None]
    target = flat_ids * (blocks * SLOTS) + block_ids * SLOTS + slot
    return target.reshape(-1).astype(jnp.int32)

def reference(tokens, norm_gain, combine, expert_ids, w_gate, w_up, w_down, d_out):
    x_float = tokens.astype(jnp.float32)
    inv_rms = lax.rsqrt(lax.optimization_barrier(jnp.mean(x_float * x_float, axis=1, keepdims=True)) + EPS)
    normed = (x_float * inv_rms * norm_gain).astype(jnp.bfloat16)
    grad_float = d_out.astype(jnp.float32)
    d_slot = (combine[:, :, None] * grad_float[:, None, :]).astype(jnp.bfloat16)
    target = row_table(expert_ids)
    per_expert = TOKENS // TOK_DEV * SLOTS
    total = EXPERTS * per_expert
    rows_in = jnp.zeros((total, D), jnp.bfloat16).at[target].set(jnp.repeat(normed, TOP, axis=0))
    grads_in = jnp.zeros((total, D), jnp.bfloat16).at[target].set(d_slot.reshape(TOKENS * TOP, D))

    def one_expert(operands):
        rows, grads, gate_w, up_w, down_w = operands
        output, d_rows, g_gate, g_up, g_down = expert_pass(rows, grads, gate_w, up_w, down_w)
        return (output.astype(jnp.bfloat16), d_rows.astype(jnp.bfloat16), g_gate.astype(jnp.bfloat16), g_up.astype(jnp.bfloat16), g_down.astype(jnp.bfloat16))
    expert_out, expert_back, d_w_gate, d_w_up, d_w_down = lax.map(one_expert, (rows_in.reshape(EXPERTS, per_expert, D), grads_in.reshape(EXPERTS, per_expert, D), w_gate, w_up, w_down))
    slot_out = expert_out.reshape(total, D)[target].astype(jnp.float32).reshape(TOKENS, TOP, D)
    slot_back = expert_back.reshape(total, D)[target].astype(jnp.float32).reshape(TOKENS, TOP, D)
    mixed = (x_float + lax.optimization_barrier(jnp.sum(combine[:, :, None] * slot_out, axis=1))).astype(jnp.bfloat16)
    d_combine = jnp.einsum('tkd,td->tk', slot_out, grad_float, precision=lax.Precision.HIGHEST)
    d_normed = lax.optimization_barrier(jnp.sum(slot_back, axis=1))
    d_gain = lax.optimization_barrier(jnp.sum(d_normed * x_float * inv_rms, axis=0))
    scaled = d_normed * norm_gain
    d_tokens = grad_float + inv_rms * scaled - x_float * inv_rms ** 3 * lax.optimization_barrier(jnp.mean(scaled * x_float, axis=1, keepdims=True))
    return (mixed, d_tokens.astype(jnp.bfloat16), d_gain, d_combine, d_w_gate, d_w_up, d_w_down)
```

```python
import jax
import jax.numpy as jnp
from jax import lax
from jax.sharding import Mesh
from jax.sharding import PartitionSpec as P

CTX = ("ctx_0", "ctx_1")
CTX_GRP = ("ctx_0", "ctx_1", "grp")
CTX_GRP_SIDE = ("ctx_0", "ctx_1", "grp", "side")

EPS = 1e-06
LANES = 128
F32 = jnp.float32
BF16 = jnp.bfloat16


def round_bf16(x):
    return lax.reduce_precision(x, 8, 7)


def dot(a, b, ca, cb):
    return lax.dot_general(a, b, (((ca,), (cb,)), ((), ())), preferred_element_type=F32)


def shifted(block, axis, step):
    n = lax.axis_size(axis)
    return lax.ppermute(block, axis, [(i, (i + step) % n) for i in range(n)])


def swapped(block):
    return lax.ppermute(block, "side", [(0, 1), (1, 0)])


def exchange(rows):
    return lax.all_to_all(rows, CTX, split_axis=0, concat_axis=0, tiled=True)


def local(tokens, norm_gain, combine, expert_ids, w_gate, w_up, w_down, d_out):
    count, width = tokens.shape
    chosen = expert_ids.shape[1]
    n_ctx = lax.axis_size(CTX)
    n_grp = lax.axis_size("grp")
    z = lax.axis_index("grp")
    slots = 2
    per_dest = n_grp * slots
    places = n_ctx * per_dest
    column = n_grp * count

    x_float = tokens.astype(F32)
    inv_rms = lax.rsqrt(jnp.mean(x_float * x_float, axis=1, keepdims=True) + EPS)
    normed = (x_float * inv_rms * norm_gain).astype(BF16)
    grad_float = d_out.astype(F32)

    high = round_bf16(combine)
    middle = round_bf16(combine - high)
    low = combine - high - middle
    pad = jnp.zeros((count, LANES - 4 * chosen), F32)
    extra = jnp.concatenate([expert_ids.astype(F32), high, middle, low, pad], axis=1)
    first = jnp.concatenate([normed, extra.astype(BF16)], axis=1)
    first_all = jnp.concatenate([first] + [shifted(first, "grp", d) for d in range(1, n_grp)], axis=0)
    second_all = jnp.concatenate([d_out] + [shifted(d_out, "grp", d) for d in range(1, n_grp)], axis=0)

    other_gate, other_up, other_down = swapped(w_gate[0]), swapped(w_up[0]), swapped(w_down[0])
    full_gate = jnp.concatenate([w_gate[0], other_gate], axis=1)
    full_up = jnp.concatenate([w_up[0], other_up], axis=1)
    full_down = jnp.concatenate([w_down[0], other_down], axis=0)

    info = first_all[:, width:].astype(F32)
    ids = info[:, :chosen]
    weights = info[:, chosen : 2 * chosen] + info[:, 2 * chosen : 3 * chosen] + info[:, 3 * chosen : 4 * chosen]
    q = jnp.arange(places, dtype=jnp.int32)
    expert_q = ((q // per_dest) * n_grp + z).astype(F32)
    block_q = (q % per_dest) // slots
    slot_q = (q % slots).astype(F32)
    t = jnp.arange(column, dtype=jnp.int32)
    same = ids[:, :, None] == expert_q[None, None, :]
    named = jnp.sum(same.astype(F32), axis=1)
    weight_q = jnp.sum(jnp.where(same, weights[:, :, None], 0.0), axis=1)
    earlier = (t[:, None] // count == t[None, :] // count) & (t[None, :] < t[:, None])
    before = dot(earlier.astype(BF16), named.astype(BF16), 1, 0)
    here = (before == slot_q[None, :]) & (t[:, None] // count == block_q[None, :])
    select = jnp.where(here, named, 0.0)
    weighted = jnp.where(here, weight_q, 0.0)
    pick = select.astype(BF16)
    slot_weight = jnp.sum(weighted, axis=0)

    send_rows = dot(pick, first_all[:, :width], 0, 0).astype(BF16)
    rows = exchange(send_rows)
    slot_grad = dot(pick, second_all, 0, 0)
    send_grads = (slot_grad * slot_weight[:, None]).astype(BF16)
    grads = exchange(send_grads)

    a_gate = dot(rows, full_gate, 1, 0)
    a_up = dot(rows, full_up, 1, 0)
    sigmoid_gate = jax.nn.sigmoid(a_gate)
    silu_gate = a_gate * sigmoid_gate
    hidden = (silu_gate * a_up).astype(BF16)
    output = dot(hidden, full_down, 1, 0).astype(BF16)
    d_hidden = dot(grads, full_down, 1, 1)
    d_up = (d_hidden * silu_gate).astype(BF16)
    d_gate = (d_hidden * a_up * sigmoid_gate * (1.0 + a_gate * (1.0 - sigmoid_gate))).astype(BF16)
    back = (dot(d_gate, full_gate, 1, 1) + dot(d_up, full_up, 1, 1)).astype(BF16)
    gain_own = jnp.sum(back.astype(F32) * rows.astype(F32), axis=0)
    gain_part = (gain_own + swapped(gain_own)).reshape(per_dest, LANES).astype(BF16)

    came_out = exchange(output)
    send_back = jnp.concatenate([back, jnp.tile(gain_part, (n_ctx, 1))], axis=1)
    came_back = exchange(send_back)

    weighted_high = round_bf16(weighted)
    stacked = jnp.concatenate([weighted_high, weighted - weighted_high], axis=0).astype(BF16)
    halves = dot(stacked, came_out, 1, 0)
    part_mixed = halves[:column] + halves[column:]
    slot_dot = jnp.sum(slot_grad * came_out.astype(F32), axis=1)
    dots = select * slot_dot[None, :]
    part_combine = jnp.sum(jnp.where(same, dots[:, None, :], 0.0), axis=2)
    combine_high = round_bf16(part_combine)
    pad = jnp.zeros((column, LANES - 2 * chosen), F32)
    part_extra = jnp.concatenate([combine_high, part_combine - combine_high, pad], axis=1)
    part_out = jnp.concatenate([part_mixed, part_extra], axis=1).astype(BF16)

    part_normed = dot(pick, came_back[:, :width], 1, 0).astype(BF16)
    gain_plane = jnp.sum(came_back[:, width:].astype(F32).reshape(n_ctx, per_dest, LANES), axis=0).astype(BF16)

    def home(blocks):
        return [blocks[0]] + [shifted(blocks[d], "grp", -d) for d in range(1, n_grp)]

    out_blocks = home([part_out[d * count : (d + 1) * count] for d in range(n_grp)])
    back_blocks = home(
        [
            jnp.concatenate([part_normed[d * count : (d + 1) * count], gain_plane], axis=1)
            for d in range(n_grp)
        ]
    )

    rows_w, grads_w, hidden_w, gate_w, up_w, _ = lax.optimization_barrier(
        (rows, grads, hidden, d_gate, d_up, came_back)
    )
    half = gate_w.shape[1] // 2
    came_gate = swapped(dot(rows_w, gate_w[:, half:], 0, 0).astype(BF16))
    came_up = swapped(dot(rows_w, up_w[:, half:], 0, 0).astype(BF16))
    came_down = swapped(dot(hidden_w[:, half:], grads_w, 0, 0).astype(BF16))
    own_gate = dot(rows_w, gate_w[:, :half], 0, 0) + came_gate.astype(F32)
    own_up = dot(rows_w, up_w[:, :half], 0, 0) + came_up.astype(F32)
    own_down = dot(hidden_w[:, :half], grads_w, 0, 0) + came_down.astype(F32)

    out_sum = sum(b.astype(F32) for b in out_blocks)
    mixed = (x_float + out_sum[:, :width]).astype(BF16)
    d_combine = out_sum[:, width : width + chosen] + out_sum[:, width + chosen : width + 2 * chosen]
    d_normed = sum(b[:, :width].astype(F32) for b in back_blocks)
    gains = jnp.stack([b[:, width:].astype(F32) for b in back_blocks])
    d_gain = jnp.sum(jnp.roll(gains, z, axis=0), axis=0).reshape(width) / norm_gain
    scaled = d_normed * norm_gain
    d_tokens = (
        grad_float
        + inv_rms * scaled
        - x_float * inv_rms**3 * jnp.mean(scaled * x_float, axis=1, keepdims=True)
    )
    return (
        mixed,
        d_tokens.astype(BF16),
        d_gain,
        d_combine,
        own_gate.astype(BF16)[None],
        own_up.astype(BF16)[None],
        own_down.astype(BF16)[None],
    )


def solution(mesh):
    split = Mesh(
        mesh.devices.reshape(4, 4, mesh.shape["grp"], mesh.shape["side"]),
        ("ctx_0", "ctx_1", "grp", "side"),
    )
    placed = (
        P(CTX_GRP_SIDE, None),
        P(),
        P(CTX_GRP_SIDE, None),
        P(CTX_GRP_SIDE, None),
        P(CTX_GRP, None, "side"),
        P(CTX_GRP, None, "side"),
        P(CTX_GRP, "side", None),
        P(CTX_GRP_SIDE, None),
    )
    return jax.shard_map(
        local,
        mesh=split,
        in_specs=placed,
        out_specs=(
            P(CTX_GRP_SIDE, None),
            P(CTX_GRP_SIDE, None),
            P(),
            P(CTX_GRP_SIDE, None),
            P(CTX_GRP, None, "side"),
            P(CTX_GRP, None, "side"),
            P(CTX_GRP, "side", None),
        ),
        check_vma=False,
    )
```

```python
import jax
import jax.numpy as jnp
from jax import lax
from jax.sharding import Mesh
from jax.sharding import PartitionSpec as P

PEERS = ("ctx_0", "ctx_1", "pair")
CTX_GRP = ("ctx_0", "ctx_1", "quad", "pair")
CTX_GRP_SIDE = ("ctx_0", "ctx_1", "quad", "pair", "side")

EPS = 1e-06
LANES = 128
F32 = jnp.float32
BF16 = jnp.bfloat16


def round_bf16(x):
    return lax.reduce_precision(x, 8, 7)


def dot(a, b, ca, cb):
    return lax.dot_general(a, b, (((ca,), (cb,)), ((), ())), preferred_element_type=F32)


def shifted(block, axis, step):
    n = lax.axis_size(axis)
    return lax.ppermute(block, axis, [(i, (i + step) % n) for i in range(n)])


def swapped(block):
    return lax.ppermute(block, "side", [(0, 1), (1, 0)])


def exchange(rows):
    return lax.all_to_all(rows, PEERS, split_axis=0, concat_axis=0, tiled=True)


def local(tokens, norm_gain, combine, expert_ids, w_gate, w_up, w_down, d_out):
    count, width = tokens.shape
    chosen = expert_ids.shape[1]
    n_quad = lax.axis_size("quad")
    n_pair = lax.axis_size("pair")
    n_peers = lax.axis_size(PEERS)
    quad = lax.axis_index("quad")
    slots = 2
    per_dest = n_quad * slots
    places = n_peers * per_dest
    column = n_quad * count

    x_float = tokens.astype(F32)
    inv_rms = lax.rsqrt(jnp.mean(x_float * x_float, axis=1, keepdims=True) + EPS)
    normed = (x_float * inv_rms * norm_gain).astype(BF16)
    grad_float = d_out.astype(F32)

    high = round_bf16(combine)
    middle = round_bf16(combine - high)
    low = combine - high - middle
    pad = jnp.zeros((count, LANES - 4 * chosen), F32)
    extra = jnp.concatenate([expert_ids.astype(F32), high, middle, low, pad], axis=1)
    block = jnp.concatenate([normed, extra.astype(BF16)], axis=1)
    gathered = jnp.concatenate([block] + [shifted(block, "quad", d) for d in range(1, n_quad)], axis=0)
    gathered_out = jnp.concatenate([d_out] + [shifted(d_out, "quad", d) for d in range(1, n_quad)], axis=0)

    other_gate, other_up, other_down = swapped(w_gate[0]), swapped(w_up[0]), swapped(w_down[0])
    full_gate = jnp.concatenate([w_gate[0], other_gate], axis=1)
    full_up = jnp.concatenate([w_up[0], other_up], axis=1)
    full_down = jnp.concatenate([w_down[0], other_down], axis=0)

    info = gathered[:, width:].astype(F32)
    ids = info[:, :chosen]
    weights = info[:, chosen : 2 * chosen] + info[:, 2 * chosen : 3 * chosen] + info[:, 3 * chosen : 4 * chosen]
    q = jnp.arange(places, dtype=jnp.int32)
    peer_q = q // per_dest
    expert_q = ((peer_q // n_pair) * (n_quad * n_pair) + quad * n_pair + peer_q % n_pair).astype(F32)
    block_q = (q % per_dest) // slots
    slot_q = (q % slots).astype(F32)
    t = jnp.arange(column, dtype=jnp.int32)
    same = ids[:, :, None] == expert_q[None, None, :]
    named = jnp.sum(same.astype(F32), axis=1)
    weight_q = jnp.sum(jnp.where(same, weights[:, :, None], 0.0), axis=1)
    earlier = (t[:, None] // count == t[None, :] // count) & (t[None, :] < t[:, None])
    before = dot(earlier.astype(BF16), named.astype(BF16), 1, 0)
    here = (before == slot_q[None, :]) & (t[:, None] // count == block_q[None, :])
    select = jnp.where(here, named, 0.0)
    weighted = jnp.where(here, weight_q, 0.0)
    pick = select.astype(BF16)
    slot_weight = jnp.sum(weighted, axis=0)

    rows = exchange(dot(pick, gathered[:, :width], 0, 0).astype(BF16))
    send_grads = (dot(pick, gathered_out, 0, 0) * slot_weight[:, None]).astype(BF16)
    rows, send_grads = lax.optimization_barrier((rows, send_grads))
    grads = exchange(send_grads)

    a_gate = dot(rows, full_gate, 1, 0)
    a_up = dot(rows, full_up, 1, 0)
    sigmoid_gate = jax.nn.sigmoid(a_gate)
    silu_gate = a_gate * sigmoid_gate
    hidden = (silu_gate * a_up).astype(BF16)
    output = dot(hidden, full_down, 1, 0).astype(BF16)
    output, grads = lax.optimization_barrier((output, grads))
    d_hidden = dot(grads, full_down, 1, 1)
    d_up = (d_hidden * silu_gate).astype(BF16)
    d_gate = (d_hidden * a_up * sigmoid_gate * (1.0 + a_gate * (1.0 - sigmoid_gate))).astype(BF16)
    back = (dot(d_gate, full_gate, 1, 1) + dot(d_up, full_up, 1, 1)).astype(BF16)
    gain_own = jnp.sum(back.astype(F32) * rows.astype(F32), axis=0)
    gain_wide = width // per_dest
    gain_rows = jnp.tile(gain_own.astype(BF16).reshape(per_dest, gain_wide), (n_peers, 1))

    came_out = exchange(output)
    send_back = jnp.concatenate([back, gain_rows], axis=1)
    returned = exchange(send_back)
    gain_peers = jnp.sum(
        returned[:, width:].astype(F32).reshape(n_peers, per_dest, gain_wide), axis=0
    )
    gain_chips = (gain_peers + swapped(gain_peers)).reshape(count, width // count).astype(BF16)

    weighted_high = round_bf16(weighted)
    stacked = jnp.concatenate([weighted_high, weighted - weighted_high], axis=0).astype(BF16)
    halves = dot(stacked, came_out, 1, 0)
    part_mixed = (halves[:column] + halves[column:]).astype(BF16)
    dots = select * dot(gathered_out, came_out, 1, 1)
    part_combine = jnp.sum(jnp.where(same, dots[:, None, :], 0.0), axis=2)
    combine_high = round_bf16(part_combine)
    pad = jnp.zeros((column, LANES - 2 * chosen), F32)
    part_extra = jnp.concatenate([combine_high, part_combine - combine_high, pad], axis=1).astype(BF16)
    part_out = jnp.concatenate([part_mixed, part_extra], axis=1)
    part_normed = dot(pick, returned[:, :width], 1, 0).astype(BF16)

    def home(block_of):
        return [block_of(0)] + [shifted(block_of(d), "quad", -d) for d in range(1, n_quad)]

    out_blocks = home(lambda d: part_out[d * count : (d + 1) * count])
    back_blocks = home(
        lambda d: jnp.concatenate([part_normed[d * count : (d + 1) * count], gain_chips], axis=1)
    )

    d_gate, d_up, hidden, _ = lax.optimization_barrier((d_gate, d_up, hidden, send_back))
    half = d_gate.shape[1] // 2
    came_gate = swapped(dot(rows, d_gate[:, half:], 0, 0).astype(BF16))
    came_up = swapped(dot(rows, d_up[:, half:], 0, 0).astype(BF16))
    came_down = swapped(dot(hidden[:, half:], grads, 0, 0).astype(BF16))
    own_gate = dot(rows, d_gate[:, :half], 0, 0) + came_gate.astype(F32)
    own_up = dot(rows, d_up[:, :half], 0, 0) + came_up.astype(F32)
    own_down = dot(hidden[:, :half], grads, 0, 0) + came_down.astype(F32)

    total = sum(b.astype(F32) for b in out_blocks)
    mixed = (x_float + total[:, :width]).astype(BF16)
    d_combine = total[:, width : width + chosen] + total[:, width + chosen : width + 2 * chosen]
    d_normed = sum(b[:, :width].astype(F32) for b in back_blocks)
    gains = jnp.stack([b[:, width:].astype(F32) for b in back_blocks])
    d_gain = jnp.sum(jnp.roll(gains, quad, axis=0), axis=0).reshape(width) / norm_gain
    scaled = d_normed * norm_gain
    d_tokens = (
        grad_float
        + inv_rms * scaled
        - x_float * inv_rms**3 * jnp.mean(scaled * x_float, axis=1, keepdims=True)
    )
    return (
        mixed,
        d_tokens.astype(BF16),
        d_gain,
        d_combine,
        own_gate.astype(BF16)[None],
        own_up.astype(BF16)[None],
        own_down.astype(BF16)[None],
    )


def solution(mesh):
    split = Mesh(
        mesh.devices.reshape(4, 4, mesh.shape["grp"] // 2, 2, mesh.shape["side"]),
        CTX_GRP_SIDE,
    )
    placed = (
        P(CTX_GRP_SIDE, None),
        P(),
        P(CTX_GRP_SIDE, None),
        P(CTX_GRP_SIDE, None),
        P(CTX_GRP, None, "side"),
        P(CTX_GRP, None, "side"),
        P(CTX_GRP, "side", None),
        P(CTX_GRP_SIDE, None),
    )
    return jax.shard_map(
        local,
        mesh=split,
        in_specs=placed,
        out_specs=(
            P(CTX_GRP_SIDE, None),
            P(CTX_GRP_SIDE, None),
            P(),
            P(CTX_GRP_SIDE, None),
            P(CTX_GRP, None, "side"),
            P(CTX_GRP, None, "side"),
            P(CTX_GRP, "side", None),
        ),
        check_vma=False,
    )
```

```python
import functools

import jax
import jax.numpy as jnp
from jax import lax
from jax.experimental import pallas as pl
from jax.experimental.pallas import tpu as pltpu
from jax.sharding import Mesh
from jax.sharding import PartitionSpec as P

PEERS = ("ctx_0", "ctx_1", "pair")
CTX_GRP = ("ctx_0", "ctx_1", "quad", "pair")
CTX_GRP_SIDE = ("ctx_0", "ctx_1", "quad", "pair", "side")

EPS = 1e-06
LANES = 128
F32 = jnp.float32
BF16 = jnp.bfloat16


def round_bf16(x):
    return lax.reduce_precision(x, 8, 7)


def dot(a, b, ca, cb):
    return lax.dot_general(a, b, (((ca,), (cb,)), ((), ())), preferred_element_type=F32)


def shifted(block, axis, step):
    n = lax.axis_size(axis)
    return lax.ppermute(block, axis, [(i, (i + step) % n) for i in range(n)])


def swapped(block):
    return lax.ppermute(block, "side", [(0, 1), (1, 0)])


def exchange(rows):
    return lax.all_to_all(rows, PEERS, split_axis=0, concat_axis=0, tiled=True)


def around(block):
    return [block] + [shifted(block, "quad", d) for d in range(1, lax.axis_size("quad"))]


def expert_body(
    per_dest, came, gate_0, gate_1, up_0, up_1, down_0, down_1, message, hidden, d_gate, d_up,
    gate, up, down, gain, sems,
):
    width = came.shape[1] // 2
    half = gate_0.shape[1]
    units = 2 * half
    copies = [
        pltpu.make_async_copy(gate_0, gate.at[:, :half], sems.at[0]),
        pltpu.make_async_copy(gate_1, gate.at[:, half:], sems.at[1]),
        pltpu.make_async_copy(up_0, up.at[:, :half], sems.at[2]),
        pltpu.make_async_copy(up_1, up.at[:, half:], sems.at[3]),
        pltpu.make_async_copy(down_0, down.at[:half, :], sems.at[4]),
        pltpu.make_async_copy(down_1, down.at[half:, :], sems.at[5]),
    ]
    for copy in copies:
        copy.start()
    step = units // 3
    for j in range(3):
        cols = slice(j * step, (j + 1) * step)
        if j == 0:
            copies[0].wait()
            copies[1].wait()
        a_gate = dot(came[:, :width], gate[:, cols], 1, 0)
        if j == 0:
            copies[2].wait()
            copies[3].wait()
        a_up = dot(came[:, :width], up[:, cols], 1, 0)
        if j == 0:
            copies[4].wait()
            copies[5].wait()
        d_hidden = dot(came[:, width:], down[cols, :], 1, 1)
        sig = jax.nn.sigmoid(a_gate)
        silu = a_gate * sig
        hidden[:, cols] = (silu * a_up).astype(BF16)
        d_up[:, cols] = (d_hidden * silu).astype(BF16)
        d_gate[:, cols] = (d_hidden * a_up * sig * (1.0 + a_gate * (1.0 - sig))).astype(BF16)
    wide = width // per_dest
    span = 2 * wide
    for j in range(width // span):
        cols = slice(j * span, (j + 1) * span)
        message[:, cols] = dot(hidden[...], down[:, cols], 1, 0).astype(BF16)
        back = (dot(d_gate[...], gate[cols, :], 1, 1) + dot(d_up[...], up[cols, :], 1, 1)).astype(BF16)
        message[:, width + j * span : width + (j + 1) * span] = back
        part = jnp.sum(back.astype(F32) * came[:, cols].astype(F32), axis=0, keepdims=True)
        gain[2 * j : 2 * j + 1, :] = part[:, :wide]
        gain[2 * j + 1 : 2 * j + 2, :] = part[:, wide:]
    rows = jnp.concatenate([gain[...], gain[...]], axis=0).astype(BF16)
    for r in range(came.shape[0] // (2 * per_dest)):
        message[2 * per_dest * r : 2 * per_dest * (r + 1), 2 * width :] = rows


def expert(came, gates, ups, downs, per_dest):
    places, both = came.shape
    width, half = gates[0].shape
    units = 2 * half
    vmem = pl.BlockSpec(memory_space=pltpu.VMEM)
    kept = pl.BlockSpec(memory_space=pltpu.HBM)
    inner = jax.ShapeDtypeStruct((places, units), BF16)
    return pl.pallas_call(
        functools.partial(expert_body, per_dest),
        out_shape=(jax.ShapeDtypeStruct((places, both + width // per_dest), BF16), inner, inner, inner),
        in_specs=[vmem] + [kept] * 6,
        out_specs=(vmem,) * 4,
        scratch_shapes=[
            pltpu.VMEM((width, units), BF16),
            pltpu.VMEM((width, units), BF16),
            pltpu.VMEM((units, width), BF16),
            pltpu.VMEM((per_dest, width // per_dest), F32),
            pltpu.SemaphoreType.DMA((6,)),
        ],
        compiler_params=pltpu.CompilerParams(vmem_limit_bytes=50 * 1024 * 1024),
        cost_estimate=pl.CostEstimate(
            flops=12 * places * width * units,
            bytes_accessed=6 * width * units + 10 * places * width,
            transcendentals=places * units,
        ),
    )(came, *gates, *ups, *downs)


def sums_body(
    per_dest, returned, pick, high, low, ids, experts, gathered, *outs,
):
    width = (returned.shape[1] // (2 * per_dest + 1)) * per_dest
    column, places = pick.shape
    count = column // len(outs)
    chosen = ids.shape[1]
    span = 512
    dots = jnp.zeros((column, places), F32)
    for j in range(width // span):
        cols = slice(j * span, (j + 1) * span)
        came_out = returned[:, cols]
        mixed = (dot(high[...], came_out, 1, 0) + dot(low[...], came_out, 1, 0)).astype(BF16)
        back = slice(width + j * span, width + (j + 1) * span)
        normed = dot(pick[...], returned[:, back], 1, 0).astype(BF16)
        dots = dots + dot(gathered[:, back], came_out, 1, 1)
        for d, out in enumerate(outs):
            out[:, cols] = mixed[d * count : (d + 1) * count]
            out[:, back] = normed[d * count : (d + 1) * count]
    dots = dots * pick[...].astype(F32)
    lane = lax.broadcasted_iota(jnp.int32, (column, LANES), 1)
    spread = jnp.zeros((column, LANES), F32)
    for k in range(chosen):
        mine = jnp.where(ids[:, k : k + 1] == experts[...], dots, 0.0)
        spread = jnp.where(lane % chosen == k, jnp.sum(mine, axis=1, keepdims=True), spread)
    upper = spread.astype(BF16).astype(F32)
    extra = jnp.where(lane < chosen, upper, jnp.where(lane < 2 * chosen, spread - upper, 0.0)).astype(BF16)
    gain = jnp.zeros((2 * per_dest, returned.shape[1] - 2 * width), F32)
    for r in range(places // (2 * per_dest)):
        gain = gain + returned[2 * per_dest * r : 2 * per_dest * (r + 1), 2 * width :].astype(F32)
    gain = gain[:per_dest] + gain[per_dest:]
    gain = jnp.concatenate([gain[:, :LANES], gain[:, LANES:]], axis=0).astype(BF16)
    for d, out in enumerate(outs):
        out[:, 2 * width : 2 * width + LANES] = extra[d * count : (d + 1) * count]
        out[:, 2 * width + LANES :] = gain


def plane_sums(per_dest, blocks, returned, pick, high, low, ids, experts, gathered):
    column, places = pick.shape
    wide = returned.shape[1]
    out = jax.ShapeDtypeStruct((column // blocks, wide), BF16)
    return pl.pallas_call(
        functools.partial(sums_body, per_dest),
        out_shape=(out,) * blocks,
        compiler_params=pltpu.CompilerParams(vmem_limit_bytes=20 * 1024 * 1024),
        cost_estimate=pl.CostEstimate(
            flops=4 * places * column * wide, bytes_accessed=2 * places * wide, transcendentals=0
        ),
    )(returned, pick, high, low, ids, experts, gathered)


def local(tokens, norm_gain, combine, expert_ids, w_gate, w_up, w_down, d_out):
    count, width = tokens.shape
    chosen = expert_ids.shape[1]
    n_quad = lax.axis_size("quad")
    n_pair = lax.axis_size("pair")
    n_peers = lax.axis_size(PEERS)
    quad = lax.axis_index("quad")
    slots = 2
    per_dest = n_quad * slots
    places = n_peers * per_dest
    column = n_quad * count

    x_float = tokens.astype(F32)
    inv_rms = lax.rsqrt(jnp.mean(x_float * x_float, axis=1, keepdims=True) + EPS)
    normed = (x_float * inv_rms * norm_gain).astype(BF16)
    grad_float = d_out.astype(F32)

    high = round_bf16(combine)
    middle = round_bf16(combine - high)
    low = combine - high - middle
    pad = jnp.zeros((count, LANES - 4 * chosen), F32)
    extra = jnp.concatenate([expert_ids.astype(F32), high, middle, low, pad], axis=1)
    block = jnp.concatenate([normed, d_out, extra.astype(BF16)], axis=1)
    gathered = jnp.concatenate(around(block), axis=0)

    other_gate, other_up, other_down = swapped(w_gate[0]), swapped(w_up[0]), swapped(w_down[0])

    info = gathered[:, 2 * width :].astype(F32)
    ids = info[:, :chosen]
    weights = info[:, chosen : 2 * chosen] + info[:, 2 * chosen : 3 * chosen] + info[:, 3 * chosen : 4 * chosen]
    q = jnp.arange(places, dtype=jnp.int32)
    peer_q = q // per_dest
    expert_q = ((peer_q // n_pair) * (n_quad * n_pair) + quad * n_pair + peer_q % n_pair).astype(F32)
    block_q = (q % per_dest) // slots
    slot_q = (q % slots).astype(F32)
    t = jnp.arange(column, dtype=jnp.int32)
    same = ids[:, :, None] == expert_q[None, None, :]
    named = jnp.sum(same.astype(F32), axis=1)
    weight_q = jnp.sum(jnp.where(same, weights[:, :, None], 0.0), axis=1)
    earlier = (t[:, None] // count == t[None, :] // count) & (t[None, :] < t[:, None])
    before = dot(earlier.astype(BF16), named.astype(BF16), 1, 0)
    here = (before == slot_q[None, :]) & (t[:, None] // count == block_q[None, :])
    select = jnp.where(here, named, 0.0)
    weighted = jnp.where(here, weight_q, 0.0)
    pick = select.astype(BF16)
    slot_weight = jnp.sum(weighted, axis=0)

    is_grad = jnp.arange(2 * width, dtype=jnp.int32) >= width
    scale = jnp.where(is_grad[None, :], slot_weight[:, None], 1.0)
    came = exchange((dot(pick, gathered[:, : 2 * width], 0, 0) * scale).astype(BF16))
    rows, grads = came[:, :width], came[:, width:]

    gain_wide = width // per_dest
    message, hidden, d_gate, d_up = expert(
        came, (w_gate[0], other_gate), (w_up[0], other_up), (w_down[0], other_down), per_dest
    )

    returned = exchange(message)
    weighted_high = round_bf16(weighted)
    blocks = plane_sums(
        per_dest, n_quad, returned, pick, weighted_high.astype(BF16),
        (weighted - weighted_high).astype(BF16), ids, expert_q[None, :], gathered,
    )
    blocks = [blocks[0]] + [shifted(blocks[d], "quad", -d) for d in range(1, n_quad)]

    half = d_gate.shape[1] // 2
    came_gate = swapped(dot(rows, d_gate[:, half:], 0, 0).astype(BF16))
    came_up = swapped(dot(rows, d_up[:, half:], 0, 0).astype(BF16))
    came_down = swapped(dot(hidden[:, half:], grads, 0, 0).astype(BF16))
    own_gate = dot(rows, d_gate[:, :half], 0, 0) + came_gate.astype(F32)
    own_up = dot(rows, d_up[:, :half], 0, 0) + came_up.astype(F32)
    own_down = dot(hidden[:, :half], grads, 0, 0) + came_down.astype(F32)

    total = sum(b[:, : 2 * width + LANES].astype(F32) for b in blocks)
    mixed = (x_float + total[:, :width]).astype(BF16)
    d_combine = total[:, 2 * width : 2 * width + chosen] + total[:, 2 * width + chosen : 2 * width + 2 * chosen]
    d_normed = total[:, width : 2 * width]
    gains = jnp.stack([b[:, 2 * width + LANES :].astype(F32) for b in blocks])
    gain_side = jnp.sum(jnp.roll(gains, quad, axis=0), axis=0)
    gain_both = gain_side + swapped(gain_side)
    d_gain = jnp.concatenate([gain_both[:per_dest], gain_both[per_dest:]], axis=1).reshape(width) / norm_gain
    scaled = d_normed * norm_gain
    d_tokens = (
        grad_float
        + inv_rms * scaled
        - x_float * inv_rms**3 * jnp.mean(scaled * x_float, axis=1, keepdims=True)
    )
    return (
        mixed,
        d_tokens.astype(BF16),
        d_gain,
        d_combine,
        own_gate.astype(BF16)[None],
        own_up.astype(BF16)[None],
        own_down.astype(BF16)[None],
    )


def solution(mesh):
    split = Mesh(
        mesh.devices.reshape(4, 4, mesh.shape["grp"] // 2, 2, mesh.shape["side"]),
        CTX_GRP_SIDE,
    )
    placed = (
        P(CTX_GRP_SIDE, None),
        P(),
        P(CTX_GRP_SIDE, None),
        P(CTX_GRP_SIDE, None),
        P(CTX_GRP, None, "side"),
        P(CTX_GRP, None, "side"),
        P(CTX_GRP, "side", None),
        P(CTX_GRP_SIDE, None),
    )
    return jax.shard_map(
        local,
        mesh=split,
        in_specs=placed,
        out_specs=(
            P(CTX_GRP_SIDE, None),
            P(CTX_GRP_SIDE, None),
            P(),
            P(CTX_GRP_SIDE, None),
            P(CTX_GRP, None, "side"),
            P(CTX_GRP, None, "side"),
            P(CTX_GRP, "side", None),
        ),
        check_vma=False,
    )
```

```python
import functools

import jax
import jax.numpy as jnp
from jax import lax
from jax.experimental import pallas as pl
from jax.experimental.pallas import tpu as pltpu
from jax.sharding import Mesh
from jax.sharding import PartitionSpec as P

PEERS = ("ctx_0", "ctx_1", "pair")
CTX_GRP = ("ctx_0", "ctx_1", "quad", "pair")
CTX_GRP_SIDE = ("ctx_0", "ctx_1", "quad", "pair", "side")

EPS = 1e-06
LANES = 128
F32 = jnp.float32
BF16 = jnp.bfloat16


def round_bf16(x):
    return lax.reduce_precision(x, 8, 7)


def dot(a, b, ca, cb):
    return lax.dot_general(a, b, (((ca,), (cb,)), ((), ())), preferred_element_type=F32)


def shifted(block, axis, step):
    n = lax.axis_size(axis)
    return lax.ppermute(block, axis, [(i, (i + step) % n) for i in range(n)])


def swapped(block):
    return lax.ppermute(block, "side", [(0, 1), (1, 0)])


def exchange(rows):
    return lax.all_to_all(rows, PEERS, split_axis=0, concat_axis=0, tiled=True)


def around(block):
    return [block] + [shifted(block, "quad", d) for d in range(1, lax.axis_size("quad"))]


def expert_body(
    per_dest, came, gate_0, gate_1, up_0, up_1, down_0, down_1, message, hidden, d_gate, d_up,
    gate, up, down, gain, sems,
):
    width = came.shape[1] // 2
    half = gate_0.shape[1]
    units = 2 * half
    copies = [
        pltpu.make_async_copy(gate_0, gate.at[:, :half], sems.at[0]),
        pltpu.make_async_copy(gate_1, gate.at[:, half:], sems.at[1]),
        pltpu.make_async_copy(up_0, up.at[:, :half], sems.at[2]),
        pltpu.make_async_copy(up_1, up.at[:, half:], sems.at[3]),
        pltpu.make_async_copy(down_0, down.at[:half, :], sems.at[4]),
        pltpu.make_async_copy(down_1, down.at[half:, :], sems.at[5]),
    ]
    for copy in copies:
        copy.start()
    step = units // 3
    for j in range(3):
        cols = slice(j * step, (j + 1) * step)
        if j == 0:
            copies[0].wait()
            copies[1].wait()
        a_gate = dot(came[:, :width], gate[:, cols], 1, 0)
        if j == 0:
            copies[2].wait()
            copies[3].wait()
        a_up = dot(came[:, :width], up[:, cols], 1, 0)
        if j == 0:
            copies[4].wait()
            copies[5].wait()
        d_hidden = dot(came[:, width:], down[cols, :], 1, 1)
        sig = jax.nn.sigmoid(a_gate)
        silu = a_gate * sig
        hidden[:, cols] = (silu * a_up).astype(BF16)
        d_up[:, cols] = (d_hidden * silu).astype(BF16)
        d_gate[:, cols] = (d_hidden * a_up * sig * (1.0 + a_gate * (1.0 - sig))).astype(BF16)
    wide = width // per_dest
    span = 2 * wide
    for j in range(width // span):
        cols = slice(j * span, (j + 1) * span)
        message[:, cols] = dot(hidden[...], down[:, cols], 1, 0).astype(BF16)
        back = (dot(d_gate[...], gate[cols, :], 1, 1) + dot(d_up[...], up[cols, :], 1, 1)).astype(BF16)
        message[:, width + j * span : width + (j + 1) * span] = back
        part = jnp.sum(back.astype(F32) * came[:, cols].astype(F32), axis=0, keepdims=True)
        gain[2 * j : 2 * j + 1, :] = part[:, :wide]
        gain[2 * j + 1 : 2 * j + 2, :] = part[:, wide:]
    rows = jnp.concatenate([gain[...], gain[...]], axis=0).astype(BF16)
    for r in range(came.shape[0] // (2 * per_dest)):
        message[2 * per_dest * r : 2 * per_dest * (r + 1), 2 * width :] = rows


def expert(came, gates, ups, downs, per_dest):
    places, both = came.shape
    width, half = gates[0].shape
    units = 2 * half
    vmem = pl.BlockSpec(memory_space=pltpu.VMEM)
    kept = pl.BlockSpec(memory_space=pltpu.HBM)
    inner = jax.ShapeDtypeStruct((places, units), BF16)
    return pl.pallas_call(
        functools.partial(expert_body, per_dest),
        out_shape=(jax.ShapeDtypeStruct((places, both + width // per_dest), BF16), inner, inner, inner),
        in_specs=[vmem] + [kept] * 6,
        out_specs=(vmem,) * 4,
        scratch_shapes=[
            pltpu.VMEM((width, units), BF16),
            pltpu.VMEM((width, units), BF16),
            pltpu.VMEM((units, width), BF16),
            pltpu.VMEM((per_dest, width // per_dest), F32),
            pltpu.SemaphoreType.DMA((6,)),
        ],
        compiler_params=pltpu.CompilerParams(vmem_limit_bytes=50 * 1024 * 1024),
        cost_estimate=pl.CostEstimate(
            flops=12 * places * width * units,
            bytes_accessed=6 * width * units + 10 * places * width,
            transcendentals=places * units,
        ),
    )(came, *gates, *ups, *downs)


def sums_body(
    per_dest, returned, pick, high, low, ids, experts, gathered, *outs,
):
    width = (returned.shape[1] // (2 * per_dest + 1)) * per_dest
    column, places = pick.shape
    count = column // len(outs)
    chosen = ids.shape[1]
    span = 512
    dots = jnp.zeros((column, places), F32)
    for j in range(width // span):
        cols = slice(j * span, (j + 1) * span)
        came_out = returned[:, cols]
        mixed = (dot(high[...], came_out, 1, 0) + dot(low[...], came_out, 1, 0)).astype(BF16)
        back = slice(width + j * span, width + (j + 1) * span)
        normed = dot(pick[...], returned[:, back], 1, 0).astype(BF16)
        dots = dots + dot(gathered[:, back], came_out, 1, 1)
        for d, out in enumerate(outs):
            out[:, cols] = mixed[d * count : (d + 1) * count]
            out[:, back] = normed[d * count : (d + 1) * count]
    dots = dots * pick[...].astype(F32)
    lane = lax.broadcasted_iota(jnp.int32, (column, LANES), 1)
    spread = jnp.zeros((column, LANES), F32)
    for k in range(chosen):
        mine = jnp.where(ids[:, k : k + 1] == experts[...], dots, 0.0)
        spread = jnp.where(lane % chosen == k, jnp.sum(mine, axis=1, keepdims=True), spread)
    upper = spread.astype(BF16).astype(F32)
    extra = jnp.where(lane < chosen, upper, jnp.where(lane < 2 * chosen, spread - upper, 0.0)).astype(BF16)
    gain = jnp.zeros((2 * per_dest, returned.shape[1] - 2 * width), F32)
    for r in range(places // (2 * per_dest)):
        gain = gain + returned[2 * per_dest * r : 2 * per_dest * (r + 1), 2 * width :].astype(F32)
    gain = gain[:per_dest] + gain[per_dest:]
    gain = jnp.concatenate([gain[:, :LANES], gain[:, LANES:]], axis=0).astype(BF16)
    for d, out in enumerate(outs):
        out[:, 2 * width : 2 * width + LANES] = extra[d * count : (d + 1) * count]
        out[:, 2 * width + LANES :] = gain


def plane_sums(per_dest, blocks, returned, pick, high, low, ids, experts, gathered):
    column, places = pick.shape
    wide = returned.shape[1]
    out = jax.ShapeDtypeStruct((column // blocks, wide), BF16)
    return pl.pallas_call(
        functools.partial(sums_body, per_dest),
        out_shape=(out,) * blocks,
        compiler_params=pltpu.CompilerParams(vmem_limit_bytes=20 * 1024 * 1024),
        cost_estimate=pl.CostEstimate(
            flops=4 * places * column * wide, bytes_accessed=2 * places * wide, transcendentals=0
        ),
    )(returned, pick, high, low, ids, experts, gathered)


def block_body(tokens_hbm, gain_hbm, out_hbm, ids_hbm, combine_hbm, block, tokens, gain, d_out, ids, combine, sems):
    width = tokens.shape[1]
    pairs = ((tokens_hbm, tokens), (ids_hbm, ids), (combine_hbm, combine), (gain_hbm, gain), (out_hbm, d_out))
    copies = [pltpu.make_async_copy(a, b, sems.at[i]) for i, (a, b) in enumerate(pairs)]
    for copy in copies:
        copy.start()
    for copy in copies:
        copy.wait()
    x = tokens[...].astype(F32)
    inv_rms = lax.rsqrt(jnp.mean(x * x, axis=1, keepdims=True) + EPS)
    block[:, :width] = (x * inv_rms * gain[...]).astype(BF16)
    block[:, width : 2 * width] = d_out[...]
    chosen = ids.shape[0]
    high = combine[...].astype(BF16)
    rest = combine[...] - high.astype(F32)
    middle = rest.astype(BF16)
    low = (rest - middle.astype(F32)).astype(BF16)
    place = lax.broadcasted_iota(jnp.int32, (chosen, LANES), 1) - lax.broadcasted_iota(
        jnp.int32, (chosen, LANES), 0
    )
    extra = jnp.zeros((tokens.shape[0], LANES), F32)
    for j, part in enumerate((ids[...].astype(F32).astype(BF16), high, middle, low)):
        extra = extra + dot(part, (place == j * chosen).astype(F32).astype(BF16), 0, 0)
    block[:, 2 * width :] = extra.astype(BF16)


def first_block(tokens, gain, d_out, ids, combine):
    count, width = tokens.shape
    args = (tokens, gain, d_out, ids, combine)
    return pl.pallas_call(
        block_body,
        out_shape=jax.ShapeDtypeStruct((count, 2 * width + LANES), BF16),
        in_specs=[pl.BlockSpec(memory_space=pltpu.HBM)] * 5,
        out_specs=pl.BlockSpec(memory_space=pltpu.VMEM),
        scratch_shapes=[pltpu.VMEM(a.shape, a.dtype) for a in args] + [pltpu.SemaphoreType.DMA((5,))],
        cost_estimate=pl.CostEstimate(flops=10**6, bytes_accessed=10**6, transcendentals=0),
    )(*args)


def local(tokens, norm_gain, combine, expert_ids, w_gate, w_up, w_down, d_out):
    count, width = tokens.shape
    chosen = expert_ids.shape[1]
    n_quad = lax.axis_size("quad")
    n_pair = lax.axis_size("pair")
    n_peers = lax.axis_size(PEERS)
    quad = lax.axis_index("quad")
    slots = 2
    per_dest = n_quad * slots
    places = n_peers * per_dest
    column = n_quad * count

    x_float = tokens.astype(F32)
    inv_rms = lax.rsqrt(jnp.mean(x_float * x_float, axis=1, keepdims=True) + EPS)
    grad_float = d_out.astype(F32)

    block = first_block(tokens, norm_gain[None, :], d_out, expert_ids.T, combine.T)
    gathered = jnp.concatenate(around(block), axis=0)

    other_gate, other_up, other_down = swapped(w_gate[0]), swapped(w_up[0]), swapped(w_down[0])

    info = gathered[:, 2 * width :].astype(F32)
    ids = info[:, :chosen]
    weights = info[:, chosen : 2 * chosen] + info[:, 2 * chosen : 3 * chosen] + info[:, 3 * chosen : 4 * chosen]
    q = jnp.arange(places, dtype=jnp.int32)
    peer_q = q // per_dest
    expert_q = ((peer_q // n_pair) * (n_quad * n_pair) + quad * n_pair + peer_q % n_pair).astype(F32)
    block_q = (q % per_dest) // slots
    slot_q = (q % slots).astype(F32)
    t = jnp.arange(column, dtype=jnp.int32)
    same = ids[:, :, None] == expert_q[None, None, :]
    named = jnp.sum(same.astype(F32), axis=1)
    weight_q = jnp.sum(jnp.where(same, weights[:, :, None], 0.0), axis=1)
    earlier = (t[:, None] // count == t[None, :] // count) & (t[None, :] < t[:, None])
    before = dot(earlier.astype(BF16), named.astype(BF16), 1, 0)
    here = (before == slot_q[None, :]) & (t[:, None] // count == block_q[None, :])
    select = jnp.where(here, named, 0.0)
    weighted = jnp.where(here, weight_q, 0.0)
    pick = select.astype(BF16)
    slot_weight = jnp.sum(weighted, axis=0)

    is_grad = jnp.arange(2 * width, dtype=jnp.int32) >= width
    scale = jnp.where(is_grad[None, :], slot_weight[:, None], 1.0)
    came = exchange((dot(pick, gathered[:, : 2 * width], 0, 0) * scale).astype(BF16))
    rows, grads = came[:, :width], came[:, width:]

    gain_wide = width // per_dest
    message, hidden, d_gate, d_up = expert(
        came, (w_gate[0], other_gate), (w_up[0], other_up), (w_down[0], other_down), per_dest
    )

    returned = exchange(message)
    weighted_high = round_bf16(weighted)
    blocks = plane_sums(
        per_dest, n_quad, returned, pick, weighted_high.astype(BF16),
        (weighted - weighted_high).astype(BF16), ids, expert_q[None, :], gathered,
    )
    blocks = [blocks[0]] + [shifted(blocks[d], "quad", -d) for d in range(1, n_quad)]

    half = d_gate.shape[1] // 2
    came_gate = swapped(dot(rows, d_gate[:, half:], 0, 0).astype(BF16))
    came_up = swapped(dot(rows, d_up[:, half:], 0, 0).astype(BF16))
    came_down = swapped(dot(hidden[:, half:], grads, 0, 0).astype(BF16))
    own_gate = dot(rows, d_gate[:, :half], 0, 0) + came_gate.astype(F32)
    own_up = dot(rows, d_up[:, :half], 0, 0) + came_up.astype(F32)
    own_down = dot(hidden[:, :half], grads, 0, 0) + came_down.astype(F32)

    total = sum(b[:, : 2 * width + LANES].astype(F32) for b in blocks)
    mixed = (x_float + total[:, :width]).astype(BF16)
    d_combine = total[:, 2 * width : 2 * width + chosen] + total[:, 2 * width + chosen : 2 * width + 2 * chosen]
    d_normed = total[:, width : 2 * width]
    gains = jnp.stack([b[:, 2 * width + LANES :].astype(F32) for b in blocks])
    gain_side = jnp.sum(jnp.roll(gains, quad, axis=0), axis=0)
    gain_both = gain_side + swapped(gain_side)
    d_gain = jnp.concatenate([gain_both[:per_dest], gain_both[per_dest:]], axis=1).reshape(width) / norm_gain
    scaled = d_normed * norm_gain
    d_tokens = (
        grad_float
        + inv_rms * scaled
        - x_float * inv_rms**3 * jnp.mean(scaled * x_float, axis=1, keepdims=True)
    )
    return (
        mixed,
        d_tokens.astype(BF16),
        d_gain,
        d_combine,
        own_gate.astype(BF16)[None],
        own_up.astype(BF16)[None],
        own_down.astype(BF16)[None],
    )


def solution(mesh):
    split = Mesh(
        mesh.devices.reshape(4, 4, mesh.shape["grp"] // 2, 2, mesh.shape["side"]),
        CTX_GRP_SIDE,
    )
    placed = (
        P(CTX_GRP_SIDE, None),
        P(),
        P(CTX_GRP_SIDE, None),
        P(CTX_GRP_SIDE, None),
        P(CTX_GRP, None, "side"),
        P(CTX_GRP, None, "side"),
        P(CTX_GRP, "side", None),
        P(CTX_GRP_SIDE, None),
    )
    return jax.shard_map(
        local,
        mesh=split,
        in_specs=placed,
        out_specs=(
            P(CTX_GRP_SIDE, None),
            P(CTX_GRP_SIDE, None),
            P(),
            P(CTX_GRP_SIDE, None),
            P(CTX_GRP, None, "side"),
            P(CTX_GRP, None, "side"),
            P(CTX_GRP, "side", None),
        ),
        check_vma=False,
    )
```
